128 devices in a mesh: seq: 16 (over z_hi, x, core), head: 8 (over z_lo, y).
Axes of the slice: x: 4, y: 4, z: 4 (z_hi: 2, z_lo: 2; z = z_hi * 2 + z_lo), core: 2. Of those that a mesh axis runs over, the one named last changes fastest.
Arguments:
- layer_input: bfloat16 [8192, 5376], P('seq'), may hold values from -6 to 6
- query: bfloat16 [8192, 4096], P('seq', 'head'), may hold values from -6 to 6
- keys: bfloat16 [8192, 2048], P('seq', 'head'), may hold values from -6 to 6
- values: bfloat16 [8192, 2048], P('seq', 'head'), may hold values from -6 to 6
- out_grad: bfloat16 [8192, 4096], P('seq', 'head'), may hold values from -6 to 6
- w_query: bfloat16 [5376, 4096], P(None, 'head'), may hold values from -0.078125 to 0.078125
- w_key: bfloat16 [5376, 2048], P(None, 'head'), may hold values from -0.078125 to 0.078125
- w_value: bfloat16 [5376, 2048], P(None, 'head'), may hold values from -0.078125 to 0.078125
- proof_lengths: int32 [16], replicated, may hold values from 1 to 2048, 8192 in all
Outputs:
- input_grad: bfloat16 [8192, 5376], P('seq', 'head')
- wq_grad: bfloat16 [5376, 4096], P('seq', 'head')
- wk_grad: bfloat16 [5376, 2048], P('seq', 'head')
- wv_grad: bfloat16 [5376, 2048], P('seq', 'head')
The draws below stay inside these ranges and needn't reach their ends.
Inputs may be any that keep to these rules, and one draw needn't show every extreme that they name: `proof_lengths`: the lengths of the 16 proofs packed in order; they sum to 8192 and the longest has exactly 2048 tokens.
All inputs are finite; a program needn't handle non-finite values.
Results may differ from the reference program's by a relative error of at most 0.015.
Values may be sent and summed in bfloat16 or wider, within the bound.
A program may use at most 128 MiB of HBM per device.

```python
import math
import jax
import jax.numpy as jnp
import numpy as np
from jax import lax

D = 5376
H = 32
KV = 16
HD = 128
WINDOW = 1024
TOK_DEV = 512
TOKENS = 8192
PROOFS = 16
MOST_LEN = 2048
N_SEQ = 16
N_HEAD = 8


def drawn_pair(key):
    base_key = jax.random.fold_in(key, 7)
    parts_keys = jax.random.split(base_key, 2)
    query_out = jnp.clip(jax.random.normal(parts_keys[0], (TOKENS, H * HD), jnp.float32), -6.0, 6.0)
    key_out = jnp.clip(jax.random.normal(parts_keys[1], (TOKENS, KV * HD), jnp.float32), -6.0, 6.0)
    return (query_out, key_out)


def draw_query(key, part):
    return drawn_pair(key)[0].astype(jnp.bfloat16)


def draw_keys(key, part):
    return drawn_pair(key)[1].astype(jnp.bfloat16)


def raised(result, key, source, target, parts, factor):
    def block_of(position):
        return (jnp.arange(result.shape[position]) // (result.shape[position] // parts)).reshape((-1,) + (1,) * (result.ndim - 1 - position))

    near = jax.random.permutation(key, parts)[block_of(target)]
    far = (block_of(target) + parts // 2) % parts
    return jnp.where((block_of(source) == near) | (block_of(source) == far), factor * result, result)


def block_levels(rng, shape, pieces, smallest, top_value):
    level = 1.0
    for axis_at, parts in pieces:
        steps = jax.random.uniform(jax.random.fold_in(jax.random.fold_in(rng, 6), axis_at), (parts,), jnp.float32, smallest / len(pieces), top_value / len(pieces))
        level = level * jnp.repeat(jnp.exp(steps), shape[axis_at] // parts).reshape((-1,) + (1,) * (len(shape) - 1 - axis_at))
    return level


def split_up(count, total, reach, lean):
    weights = [(1 << 20) // math.isqrt(standing ** lean) + 1 for standing in range(2, count + 1)]
    surplus, holding = total - reach - (count - 1), [1] * (count - 1)
    while surplus > 0:
        candidates = [i for i in range(count - 1) if holding[i] < reach]
        mass, budget = sum([weights[i] for i in candidates]), surplus
        for i in candidates:
            extra = min(reach - holding[i], max(1, budget * weights[i] // mass), surplus)
            holding[i] = holding[i] + extra
            surplus = surplus - extra
    return np.array([reach] + holding)


def ragged(key, count, total, most, slope):
    if count == 2:
        one = jax.random.randint(key, (), max(1, total - most), min(most, total - 1) + 1)
        return jnp.stack([one, total - one])
    tallies = jnp.asarray(split_up(count, total, most, slope), jnp.int32)
    pairs = (count - 1) // 2
    source_of, sink = tallies[1:1 + 2 * pairs:2], tallies[2:2 + 2 * pairs:2]
    margin = jnp.minimum(source_of - 1, most - sink)
    moved = jax.random.randint(jax.random.fold_in(key, 1), (pairs,), 0, 1 << 20) % (margin + 1)
    tallies = tallies.at[1:1 + 2 * pairs:2].set(source_of - moved).at[2:2 + 2 * pairs:2].set(sink + moved)
    return tallies[jax.random.permutation(jax.random.fold_in(key, 2), count)]


def normal_values(own_key, extent, scale, limit, cuts=(), kind=jnp.bfloat16):
    values = scale * jax.random.normal(own_key, extent, jnp.float32)
    if cuts:
        values = values * block_levels(own_key, extent, cuts, -0.22, 0.18)
    return jnp.clip(values, -limit, limit).astype(kind)


def bell_draw_with(stream_key, shape, spread, most, shards, heavy, kind=jnp.bfloat16):
    entries = spread * jax.random.normal(stream_key, shape, jnp.float32)
    if shards:
        entries = entries * block_levels(stream_key, shape, shards, -0.22, 0.18)
    return jnp.clip(raised(entries, jax.random.fold_in(stream_key, 3), *heavy), -most, most).astype(kind)


def setup_inputs(seed: int = 0) -> dict:
    arg_keys = jax.random.split(jax.random.key(seed), 10)
    return {
        "layer_input": bell_draw_with(arg_keys[0], (TOKENS, D), 1.0, 6.0, ((0, 16),), (0, 1, 16, 2.0)),
        "query": draw_query(jax.random.fold_in(arg_keys[9], 71), 0),
        "keys": draw_keys(jax.random.fold_in(arg_keys[9], 71), 0),
        "values": normal_values(arg_keys[3], (TOKENS, KV * HD), 1.0, 6.0, ((0, 16), (1, 8))),
        "out_grad": normal_values(arg_keys[4], (TOKENS, H * HD), 1.0, 6.0, ((0, 16), (1, 8))),
        "w_query": normal_values(arg_keys[5], (D, H * HD), D ** -0.5, 0.078125, ((1, 8),)),
        "w_key": normal_values(arg_keys[6], (D, KV * HD), D ** -0.5, 0.078125, ((1, 8),)),
        "w_value": normal_values(arg_keys[7], (D, KV * HD), D ** -0.5, 0.078125, ((1, 8),)),
        "proof_lengths": ragged(arg_keys[8], PROOFS, TOKENS, MOST_LEN, 2).astype(jnp.int32),
    }


def proof_index(positions, proof_lengths):
    lengths_sum = jnp.cumsum(proof_lengths).astype(jnp.int32)
    starts_at = (lengths_sum - proof_lengths).astype(jnp.int32)
    counted = jnp.sum((positions[:, None] >= starts_at[None, :]).astype(jnp.int32), axis=1)
    return (counted - 1).astype(jnp.int32)


def build_mask(query_pos, key_pos, query_seg, key_seg):
    before = key_pos[None, :] <= query_pos[:, None]
    inside = query_pos[:, None] - key_pos[None, :] < WINDOW
    present = key_pos[None, :] >= 0
    same_proof = query_seg[:, None] == key_seg[None, :]
    return before & inside & present & same_proof


def rounded(value):
    return lax.optimization_barrier(value.astype(jnp.bfloat16)).astype(jnp.float32)


def block_grads(q_block, k_block, v_block, g_block, pair_mask, score_scale):
    scores = jnp.einsum("qkgd,lkd->kgql", q_block, k_block) * score_scale
    scores = jnp.where(pair_mask, scores, -1e30)
    row_max = jnp.max(scores, axis=-1, keepdims=True)
    weights_exp = jnp.where(pair_mask, jnp.exp(scores - row_max), 0.0)
    probs_full = weights_exp / jnp.sum(weights_exp, axis=-1, keepdims=True)
    probs_low = rounded(probs_full)
    attn_out = jnp.einsum("kgql,lkd->qkgd", probs_low, v_block)
    row_delta = jnp.einsum("qkgd,qkgd->kgq", g_block, attn_out)
    prob_grad = jnp.einsum("qkgd,lkd->kgql", g_block, v_block)
    score_low = rounded(probs_full * (prob_grad - row_delta[..., None]))
    query_grad = (score_scale * jnp.einsum("kgql,lkd->qkgd", score_low, k_block)).astype(jnp.bfloat16)
    key_grad = score_scale * jnp.einsum("kgql,qkgd->lkd", score_low, q_block)
    value_grad = jnp.einsum("kgql,qkgd->lkd", probs_low, g_block)
    return query_grad, key_grad, value_grad


def product_t(left, right):
    return jnp.dot(left.astype(jnp.float32), right.astype(jnp.float32).T, preferred_element_type=jnp.float32)


def reference(layer_input, query, keys, values, out_grad, w_query, w_key, w_value, proof_lengths):
    groups = H // KV
    score_scale = (D // H) ** -0.5
    block_rows = math.gcd(TOKENS, 512)
    span_rows = block_rows + WINDOW
    positions = jnp.arange(TOKENS, dtype=jnp.int32)
    segment_all = proof_index(positions, proof_lengths)
    padded_keys = jnp.concatenate([jnp.zeros((WINDOW, KV * HD), keys.dtype), keys], axis=0)
    padded_values = jnp.concatenate([jnp.zeros((WINDOW, KV * HD), values.dtype), values], axis=0)
    padded_segments = jnp.concatenate([jnp.full((WINDOW,), -1, jnp.int32), segment_all])

    def one_block(carry, block_index):
        key_acc, value_acc = carry
        first_row = (block_index * block_rows).astype(jnp.int32)
        q_block = lax.dynamic_slice_in_dim(query, first_row, block_rows, 0).astype(jnp.float32).reshape(block_rows, KV, groups, HD)
        g_block = lax.dynamic_slice_in_dim(out_grad, first_row, block_rows, 0).astype(jnp.float32).reshape(block_rows, KV, groups, HD)
        k_block = lax.dynamic_slice_in_dim(padded_keys, first_row, span_rows, 0).astype(jnp.float32).reshape(span_rows, KV, HD)
        v_block = lax.dynamic_slice_in_dim(padded_values, first_row, span_rows, 0).astype(jnp.float32).reshape(span_rows, KV, HD)
        query_pos = first_row + jnp.arange(block_rows, dtype=jnp.int32)
        key_pos = first_row - WINDOW + jnp.arange(span_rows, dtype=jnp.int32)
        query_seg = lax.dynamic_slice_in_dim(segment_all, first_row, block_rows, 0)
        key_seg = lax.dynamic_slice_in_dim(padded_segments, first_row, span_rows, 0)
        pair_mask = build_mask(query_pos, key_pos, query_seg, key_seg)
        q_grad, k_grad, v_grad = block_grads(q_block, k_block, v_block, g_block, pair_mask, score_scale)
        key_acc = lax.dynamic_update_slice_in_dim(key_acc, lax.dynamic_slice_in_dim(key_acc, first_row, span_rows, 0) + k_grad, first_row, 0)
        value_acc = lax.dynamic_update_slice_in_dim(value_acc, lax.dynamic_slice_in_dim(value_acc, first_row, span_rows, 0) + v_grad, first_row, 0)
        return (key_acc, value_acc), q_grad.reshape(block_rows, H * HD)

    start_acc = jnp.zeros((TOKENS + WINDOW, KV, HD), jnp.float32)
    block_ids = jnp.arange(TOKENS // block_rows, dtype=jnp.int32)
    (key_acc, value_acc), query_parts = lax.scan(one_block, (start_acc, start_acc), block_ids)
    query_grad = query_parts.reshape(TOKENS, H * HD)
    key_grad = key_acc[WINDOW:].reshape(TOKENS, KV * HD).astype(jnp.bfloat16)
    value_grad = value_acc[WINDOW:].reshape(TOKENS, KV * HD).astype(jnp.bfloat16)

    q_cols = H * HD // N_HEAD
    k_cols = KV * HD // N_HEAD
    input_sum = jnp.zeros((TOKENS, D), jnp.float32)
    for member in range(N_HEAD):
        q_lower = member * q_cols
        k_lower = member * k_cols
        head_term = product_t(query_grad[:, q_lower:q_lower + q_cols], w_query[:, q_lower:q_lower + q_cols])
        head_term = head_term + product_t(key_grad[:, k_lower:k_lower + k_cols], w_key[:, k_lower:k_lower + k_cols])
        head_term = head_term + product_t(value_grad[:, k_lower:k_lower + k_cols], w_value[:, k_lower:k_lower + k_cols])
        input_sum = input_sum + rounded(head_term)
    input_grad = input_sum.astype(jnp.bfloat16)

    all_grads = jnp.concatenate([query_grad, key_grad, value_grad], axis=1)

    def seq_term(carry, member):
        first_row = (member * TOK_DEV).astype(jnp.int32)
        inputs_part = lax.dynamic_slice_in_dim(layer_input, first_row, TOK_DEV, 0).astype(jnp.float32)
        grads_part = lax.dynamic_slice_in_dim(all_grads, first_row, TOK_DEV, 0).astype(jnp.float32)
        term = jnp.dot(inputs_part.T, grads_part, preferred_element_type=jnp.float32)
        return carry + rounded(term), None

    weight_total, _ = lax.scan(seq_term, jnp.zeros((D, (H + 2 * KV) * HD), jnp.float32), jnp.arange(N_SEQ, dtype=jnp.int32))
    wq_grad = weight_total[:, :H * HD].astype(jnp.bfloat16)
    wk_grad = weight_total[:, H * HD:H * HD + KV * HD].astype(jnp.bfloat16)
    wv_grad = weight_total[:, H * HD + KV * HD:].astype(jnp.bfloat16)
    return (input_grad, wq_grad, wk_grad, wv_grad)
```

```python
import functools
import math

import jax
import jax.numpy as jnp
from jax import lax
from jax.experimental import pallas as pl
from jax.experimental.pallas import tpu as pltpu
from jax.sharding import PartitionSpec as P

D = 5376
H = 32
HD = 128
WINDOW = 1024
ROWS = 512
BLOCK = 128
SPAN = WINDOW + BLOCK
EXT = WINDOW + ROWS
SCALE = (D // H) ** -0.5
EXP2_SCALE = SCALE * math.log2(math.e)
F32 = jnp.float32
BF16 = jnp.bfloat16
PIECE = 336
MESH = pl.DeviceIdType.MESH

NN = (((1,), (0,)), ((), ()))
NT = (((1,), (1,)), ((), ()))


def dot(left, right, dims):
    return lax.dot_general(left, right, dims, preferred_element_type=F32)


def attention_kernel(
    lengths, q, g, k2, k1, k0, v2, v1, v0,
    dq, dk2, dk1, dk0, dv2, dv1, dv0,
    keys, values, bias, dk_acc, dv_acc,
):
    first_row = lax.axis_index("seq") * ROWS
    for part, (k, v) in enumerate(((k2, v2), (k1, v1), (k0, v0))):
        keys[part * ROWS:(part + 1) * ROWS, :] = k[...]
        values[part * ROWS:(part + 1) * ROWS, :] = v[...]
    dk_acc[...] = jnp.zeros_like(dk_acc)
    dv_acc[...] = jnp.zeros_like(dv_acc)

    def block(b, carry):
        i0 = pl.multiple_of(b * BLOCK, BLOCK)
        row = lax.broadcasted_iota(jnp.int32, (BLOCK, 1), 0)
        position = first_row + i0 + row
        start = jnp.zeros((BLOCK, 1), jnp.int32)
        proof_start = jnp.int32(0)
        for proof in range(lengths.shape[0]):
            start = jnp.maximum(start, jnp.where(position >= proof_start, proof_start, 0))
            proof_start = proof_start + lengths[proof]
        lowest = jnp.maximum(start, position - (WINDOW - 1))
        lowest = lowest - (first_row - WINDOW) - i0
        column = lax.broadcasted_iota(jnp.int32, (BLOCK, SPAN), 1)
        seen = (column >= lowest) & (column <= row + WINDOW)
        bias[...] = jnp.where(seen, 0.0, -1e30).astype(F32)
        rows = pl.ds(i0, BLOCK)
        span = pl.ds(i0, SPAN)
        for kv in range(2):
            lanes = slice(kv * HD, (kv + 1) * HD)
            heads = (slice(2 * kv * HD, (2 * kv + 1) * HD), slice((2 * kv + 1) * HD, (2 * kv + 2) * HD))
            q2 = jnp.concatenate([q[rows, h] for h in heads], axis=0)
            g2 = jnp.concatenate([g[rows, h] for h in heads], axis=0)
            k = keys[span, lanes]
            v = values[span, lanes]
            both = jnp.concatenate([bias[...], bias[...]], axis=0)
            scores = dot(q2, k, NT) + both
            top = jnp.max(scores, axis=1, keepdims=True)
            weight = jnp.exp2((scores - top) * EXP2_SCALE)
            probs = weight * (1.0 / jnp.sum(weight, axis=1, keepdims=True))
            low = probs.astype(BF16)
            prob_grad = dot(g2, v, NT)
            delta = jnp.sum(low.astype(F32) * prob_grad, axis=1, keepdims=True)
            score_low = (probs * (prob_grad - delta)).astype(BF16)
            query_grad = (dot(score_low, k, NN) * SCALE).astype(BF16)
            dq[rows, heads[0]] = query_grad[:BLOCK]
            dq[rows, heads[1]] = query_grad[BLOCK:]
            dk_acc[kv, :, span] += dot(q2.T, score_low, NN)
            dv_acc[kv, :, span] += dot(g2.T, low, NN)
        return carry

    lax.fori_loop(0, ROWS // BLOCK, block, 0)
    for kv in range(2):
        lanes = slice(kv * HD, (kv + 1) * HD)
        for part, (dk, dv) in enumerate(((dk2, dv2), (dk1, dv1), (dk0, dv0))):
            cols = slice(part * ROWS, (part + 1) * ROWS)
            dk[lanes, :] = (dk_acc[kv, :, cols] * SCALE).astype(dk.dtype)
            dv[lanes, :] = dv_acc[kv, :, cols].astype(dv.dtype)


def attention(lengths, q, g, k, v):
    vmem = pl.BlockSpec(memory_space=pltpu.VMEM)
    shape = (2 * HD, ROWS)
    sums = [jax.ShapeDtypeStruct(shape, t) for t in (BF16, BF16, F32)]
    return pl.pallas_call(
        attention_kernel,
        out_shape=[jax.ShapeDtypeStruct(q.shape, BF16)] + sums + sums,
        in_specs=[pl.BlockSpec(memory_space=pltpu.SMEM)] + [vmem] * 8,
        out_specs=[vmem] * 7,
        scratch_shapes=[
            pltpu.VMEM((EXT, 2 * HD), BF16),
            pltpu.VMEM((EXT, 2 * HD), BF16),
            pltpu.VMEM((BLOCK, SPAN), F32),
            pltpu.VMEM((2, HD, EXT), F32),
            pltpu.VMEM((2, HD, EXT), F32),
        ],
        compiler_params=pltpu.CompilerParams(vmem_limit_bytes=40 << 20),
        cost_estimate=pl.CostEstimate(flops=4 << 30, bytes_accessed=4 << 20, transcendentals=3 << 20),
        name="attention",
    )(lengths, q, g, *k, *v)


def coordinates():
    seq = lax.axis_index("seq")
    head = lax.axis_index("head")
    core, x, zh = seq % 2, (seq // 2) % 4, seq // 8
    y, zl = head % 4, head // 4

    def at(zh_, x_, core_, zl_, y_):
        return {"seq": zh_ * 8 + x_ * 2 + core_, "head": zl_ * 4 + y_}

    mate = at(zh, x, 1 - core, zl, y)
    right = (at(zh, (x + 1) % 4, core, zl, y), at(zh, x, core, zl, (y + 1) % 4))
    left = (at(zh, (x + 3) % 4, core, zl, y), at(zh, x, core, zl, (y + 3) % 4))
    across = (at(1 - zh, x, core, zl, y), at(zh, x, core, 1 - zl, y))
    return core, (x, y), (zh, zl), mate, right, left, across


def reduce_kernel(
    xt, wq, wk, wv, dq, dk, dv,
    out_h, out_q, out_k, out_v,
    x_own, wq_own, wk_own, wv_own, dq_all, dk_all, dv_all,
    part, relay, final, zland,
    load_sem, own_sem, mate_send, mate_recv, send_sem, recv_sem,
):
    core, place, depth, mate, right, left, across = coordinates()
    barrier = pltpu.get_barrier_semaphore()
    peers = (mate,) + right + left + across
    for peer in peers:
        pl.semaphore_signal(barrier, inc=1, device_id=peer, device_id_type=MESH)

    mine = pl.ds(pl.multiple_of(core * ROWS, ROWS), ROWS)
    other = 1 - core

    def target(axis, t):
        side, u = t // 4, t % 4
        off = 2 - u + (u // 2) * 3 - (u // 3) * 2
        z = (1 - depth[axis] + side) % 2
        return z * 4 + (place[axis] + off) % 4

    def weight_loads(t):
        h = target(1, t)
        return [
            pltpu.make_async_copy(wq.at[h], wq_own.at[t], load_sem.at[0, t]),
            pltpu.make_async_copy(wk.at[h], wk_own.at[t], load_sem.at[1, t]),
            pltpu.make_async_copy(wv.at[h], wv_own.at[t], load_sem.at[2, t]),
        ]

    def own_loads():
        return [
            pltpu.make_async_copy(dq, dq_all.at[mine, :], own_sem.at[0]),
            pltpu.make_async_copy(dk, dk_all.at[:, mine], own_sem.at[1]),
            pltpu.make_async_copy(dv, dv_all.at[:, mine], own_sem.at[2]),
        ]

    def x_load(t):
        s = target(0, t)
        return pltpu.make_async_copy(xt.at[2 * s + core], x_own.at[t, :, mine], load_sem.at[3, t])

    for copy in own_loads():
        copy.start()
    for t in range(8):
        for copy in weight_loads(t):
            copy.start()
        x_load(t).start()

    def remote(src, dst, send, recv, device):
        return pltpu.make_async_remote_copy(
            src_ref=src, dst_ref=dst, send_sem=send, recv_sem=recv,
            device_id=device, device_id_type=MESH,
        )

    def mate_grads():
        return [
            remote(dq, dq_all.at[mine, :], mate_send.at[0], mate_recv.at[0], mate),
            remote(dk, dk_all.at[:, mine], mate_send.at[1], mate_recv.at[1], mate),
            remote(dv, dv_all.at[:, mine], mate_send.at[2], mate_recv.at[2], mate),
        ]

    def mate_x(t):
        s = target(0, t)
        return remote(
            xt.at[2 * s + other], x_own.at[t, :, mine], mate_send.at[3 + t], mate_recv.at[3 + t], mate
        )

    pl.semaphore_wait(barrier, len(peers))
    for copy in mate_grads():
        copy.start()
    for t in range(8):
        mate_x(t).start()

    def hop(axis, n, src, dst, device):
        return remote(src, dst, send_sem.at[axis, n], recv_sem.at[axis, n], device)

    def opposite(axis, side, way):
        device = (right, left)[way][axis]
        return hop(axis, 7 * side + way, part.at[axis, side, 0, way], relay.at[axis, side, way], device)

    def plain(axis, side, way):
        device = (right, left)[way][axis]
        half = 1 - way
        return hop(
            axis, 7 * side + 2 + way, part.at[axis, side, 1 + way, half], final.at[axis, side, way, half], device
        )

    def summed(axis, side, way):
        device = (right, left)[way][axis]
        half = way
        return hop(
            axis, 7 * side + 4 + way, part.at[axis, side, 1 + way, half], final.at[axis, side, way, half], device
        )

    def crossing(axis, half):
        return hop(axis, (6, 13)[half], part.at[axis, 0, 3, half], zland.at[axis, half], across[axis])

    def forward(side):
        for axis in range(2):
            for way in range(2):
                opposite(axis, side, way).wait_recv()
                kept = part[axis, side, 1 + way, way].astype(F32)
                part[axis, side, 1 + way, way] = (kept + relay[axis, side, way].astype(F32)).astype(BF16)
                summed(axis, side, way).start()

    def collected(axis, side, half):
        total = part[axis, side, 3, half].astype(F32)
        return total + final[axis, side, 0, half].astype(F32) + final[axis, side, 1, half].astype(F32)

    for copy in own_loads():
        copy.wait()

    def step(t, carry):
        side, u = t // 4, t % 4
        for copy in weight_loads(t):
            copy.wait()
        x_load(t).wait()
        for half in range(2):
            product = dot(wq_own[t, half], dq_all[mine, :], NT)
            product += dot(wk_own[t, half], dk_all[:, mine], NN)
            product += dot(wv_own[t, half], dv_all[:, mine], NN)
            part[1, side, u, half] = product.astype(BF16)

        @pl.when(t == 0)
        def _():
            for copy in mate_grads():
                copy.wait()

        mate_x(t).wait()
        part[0, side, u, 0] = dot(x_own[t], dq_all[...], NN).astype(BF16)
        part[0, side, u, 1, :, : 2 * HD] = dot(x_own[t], dk_all[...], NT).astype(BF16)
        part[0, side, u, 1, :, 2 * HD:] = dot(x_own[t], dv_all[...], NT).astype(BF16)

        for now in range(2):
            @pl.when(t == 4 * now)
            def _():
                if now == 1:
                    forward(0)
                for axis in range(2):
                    for way in range(2):
                        opposite(axis, now, way).start()

            for way in range(2):
                @pl.when(t == 4 * now + 1 + way)
                def _():
                    for axis in range(2):
                        plain(axis, now, way).start()

        return carry

    lax.fori_loop(0, 8, step, 0)

    for axis in range(2):
        for way in range(2):
            plain(axis, 0, way).wait_recv()
            summed(axis, 0, way).wait_recv()
        for half in range(2):
            part[axis, 0, 3, half] = collected(axis, 0, half).astype(BF16)
            crossing(axis, half).start()
    forward(1)
    for axis in (1, 0):
        for way in range(2):
            plain(axis, 1, way).wait_recv()
            summed(axis, 1, way).wait_recv()
        for half in range(2):
            crossing(axis, half).wait_recv()
        result = [collected(axis, 1, half) + zland[axis, half].astype(F32) for half in range(2)]
        if axis == 1:
            out_h[...] = jnp.concatenate(result, axis=0).T.astype(BF16)
        else:
            out_q[...] = result[0].astype(BF16)
            out_k[...] = result[1][:, : 2 * HD].astype(BF16)
            out_v[...] = result[1][:, 2 * HD:].astype(BF16)
    for axis in range(2):
        for side in range(2):
            for way in range(2):
                opposite(axis, side, way).wait_send()
                plain(axis, side, way).wait_send()
                summed(axis, side, way).wait_send()
            crossing(axis, side).wait_send()


def reduced(xt, wq, wk, wv, dq, dk, dv):
    vmem = pl.BlockSpec(memory_space=pltpu.VMEM)
    anywhere = pl.BlockSpec(memory_space=pl.ANY)
    cols = 4 * HD
    dma = pltpu.SemaphoreType.DMA
    return pl.pallas_call(
        reduce_kernel,
        out_shape=[
            jax.ShapeDtypeStruct((ROWS, 2 * PIECE), BF16),
            jax.ShapeDtypeStruct((PIECE, cols), BF16),
            jax.ShapeDtypeStruct((PIECE, cols // 2), BF16),
            jax.ShapeDtypeStruct((PIECE, cols // 2), BF16),
        ],
        in_specs=[anywhere] * 4 + [vmem] * 3,
        out_specs=[vmem] * 4,
        scratch_shapes=[
            pltpu.VMEM((8, PIECE, 2 * ROWS), BF16),
            pltpu.VMEM((8, 2, PIECE, cols), BF16),
            pltpu.VMEM((8, 2, PIECE, cols // 2), BF16),
            pltpu.VMEM((8, 2, PIECE, cols // 2), BF16),
            pltpu.VMEM((2 * ROWS, cols), BF16),
            pltpu.VMEM((cols // 2, 2 * ROWS), BF16),
            pltpu.VMEM((cols // 2, 2 * ROWS), BF16),
            pltpu.VMEM((2, 2, 4, 2, PIECE, cols), BF16),
            pltpu.VMEM((2, 2, 2, PIECE, cols), BF16),
            pltpu.VMEM((2, 2, 2, 2, PIECE, cols), BF16),
            pltpu.VMEM((2, 2, PIECE, cols), BF16),
            dma((4, 8)),
            dma((3,)),
            dma((11,)),
            dma((11,)),
            dma((2, 14)),
            dma((2, 14)),
        ],
        compiler_params=pltpu.CompilerParams(
            collective_id=1, has_side_effects=True, vmem_limit_bytes=56 << 20
        ),
        name="reduce",
    )(xt, wq, wk, wv, dq, dk, dv)


def shifted(block, distance):
    devices = range(lax.axis_size("seq"))
    route = [(i - distance, i) for i in devices if i - distance in devices]
    return lax.ppermute(block, "seq", route)


def on_device(layer_input, query, keys, values, out_grad, w_query, w_key, w_value, proof_lengths):
    xt = layer_input.T.reshape(16, PIECE, ROWS)
    k = [shifted(keys, 2), shifted(keys, 1), keys]
    v = [shifted(values, 2), shifted(values, 1), values]
    dq, dk2, dk1, dk0, dv2, dv1, dv0 = attention(proof_lengths, query, out_grad, k, v)
    dk = dk0 + shifted(dk1, -1).astype(F32) + shifted(dk2, -2).astype(F32)
    dv = dv0 + shifted(dv1, -1).astype(F32) + shifted(dv2, -2).astype(F32)
    return tuple(
        reduced(
            xt,
            w_query.reshape(8, 2, PIECE, -1),
            w_key.reshape(8, 2, PIECE, -1),
            w_value.reshape(8, 2, PIECE, -1),
            dq,
            dk.astype(BF16),
            dv.astype(BF16),
        )
    )


def solution(mesh):
    return jax.shard_map(
        on_device,
        mesh=mesh,
        in_specs=(
            P("seq", None),
            P("seq", "head"),
            P("seq", "head"),
            P("seq", "head"),
            P("seq", "head"),
            P(None, "head"),
            P(None, "head"),
            P(None, "head"),
            P(),
        ),
        out_specs=(P("seq", "head"), P("seq", "head"), P("seq", "head"), P("seq", "head")),
        check_vma=False,
    )
```

```python
import math

import jax
import jax.numpy as jnp
from jax import lax
from jax.experimental import pallas as pl
from jax.experimental.pallas import tpu as pltpu
from jax.sharding import PartitionSpec as P

D = 5376
H = 32
HD = 128
WINDOW = 1024
ROWS = 512
BLOCK = 128
SPAN = WINDOW + BLOCK
EXT = WINDOW + ROWS
SCALE = (D // H) ** -0.5
EXP2_SCALE = SCALE * math.log2(math.e)
F32 = jnp.float32
BF16 = jnp.bfloat16
PIECE = 336
CUT = 176
COLS = 512
MESH = pl.DeviceIdType.MESH

NN = (((1,), (0,)), ((), ()))
NT = (((1,), (1,)), ((), ()))

WEIGHT, INPUT = 0, 1
WAY_ROWS = (slice(0, CUT), slice(CUT, PIECE))


def dot(left, right, dims):
    return lax.dot_general(left, right, dims, preferred_element_type=F32)


def row_bias(lengths, first_row, i0):
    row = lax.broadcasted_iota(jnp.int32, (BLOCK, 1), 0)
    position = first_row + i0 + row
    start = jnp.zeros((BLOCK, 1), jnp.int32)
    proof_start = jnp.int32(0)
    for proof in range(lengths.shape[0]):
        start = jnp.maximum(start, jnp.where(position >= proof_start, proof_start, 0))
        proof_start = proof_start + lengths[proof]
    lowest = jnp.maximum(start, position - (WINDOW - 1))
    lowest = lowest - (first_row - WINDOW) - i0
    column = lax.broadcasted_iota(jnp.int32, (BLOCK, SPAN), 1)
    seen = (column >= lowest) & (column <= row + WINDOW)
    return jnp.where(seen, 0.0, -1e30).astype(F32)


def step_kernel(
    lengths, x, q_in, g_in, k_in, v_in, wq_in, wk_in, wv_in,
    out_h, out_q, out_kv,
    x_nat, xt, x_mate, q, g, keys, values, wq, wkv, bias, dk_acc, dv_acc,
    dq, dq_mate, dkv, dkv_mate, halo_out, halo_in,
    part, relay, final, zland, zrelay,
    load_sem, kv_send, kv_recv, gh_send, gh_recv, mate_send, mate_recv, send_sem, recv_sem,
):
    seq = lax.axis_index("seq")
    head = lax.axis_index("head")
    core, px, zh = seq % 2, (seq // 2) % 4, seq // 8
    py, zl = head % 4, head // 4
    zz = zh * 2 + zl

    def at(z_, x_, core_, y_):
        return {"seq": (z_ // 2) * 8 + x_ * 2 + core_, "head": (z_ % 2) * 4 + y_}

    mate = at(zz, px, 1 - core, py)
    right = (at(zz, (px + 1) % 4, core, py), at(zz, px, core, (py + 1) % 4))
    left = (at(zz, (px + 3) % 4, core, py), at(zz, px, core, (py + 3) % 4))
    above = at((zz + 1) % 4, px, core, py)
    below = at((zz + 3) % 4, px, core, py)
    beside = at(zh * 2 + 1 - zl, px, core, py)
    later = [{"seq": (seq + n) % 16, "head": head} for n in (1, 2)]
    earlier = [{"seq": (seq + 16 - n) % 16, "head": head} for n in (1, 2)]
    place, depth = (px, py), (zh, zl)

    barrier = pltpu.get_barrier_semaphore()
    peers = tuple(later) + tuple(earlier) + right + left + (above, below)
    for peer in peers:
        pl.semaphore_signal(barrier, inc=1, device_id=peer, device_id_type=MESH)

    places = (
        (q_in, q),
        (g_in, g),
        (k_in, keys.at[WINDOW:EXT, :]),
        (v_in, values.at[WINDOW:EXT, :]),
        (x, x_nat),
        (wq_in, wq),
        (wk_in, wkv.at[:, :, : 2 * HD]),
        (wv_in, wkv.at[:, :, 2 * HD:]),
    )

    def load(n):
        return pltpu.make_async_copy(*places[n], load_sem.at[n])

    for n in range(8):
        load(n).start()

    def remote(src, dst, send, recv, device):
        return pltpu.make_async_remote_copy(
            src_ref=src, dst_ref=dst, send_sem=send, recv_sem=recv,
            device_id=device, device_id_type=MESH,
        )

    def kv_copy(kv, n, which):
        src, dst = ((k_in, keys), (v_in, values))[which]
        lanes = slice(kv * HD, (kv + 1) * HD)
        rows = slice(WINDOW - (n + 1) * ROWS, WINDOW - n * ROWS)
        return remote(
            src.at[:, lanes], dst.at[rows, lanes],
            kv_send.at[kv, n, which], kv_recv.at[kv, n, which], later[n],
        )

    def grad_copy(kv, n, which):
        return remote(
            halo_out.at[kv, n, which], halo_in.at[kv, n, which],
            gh_send.at[kv, n, which], gh_recv.at[kv, n, which], earlier[n],
        )

    def mate_copy(n, src, dst):
        return remote(src, dst, mate_send.at[n], mate_recv.at[n], mate)

    def block_rows(index):
        return pl.ds(pl.multiple_of(index * PIECE, 16), PIECE)

    def mate_x(j):
        return mate_copy(j, xt.at[block_rows(2 * j + 1 - core), :], x_mate.at[j])

    def mate_dq(kv):
        lanes = slice(kv * 2 * HD, (kv + 1) * 2 * HD)
        return mate_copy(8 + kv, dq.at[:, lanes], dq_mate.at[:, lanes])

    def mate_dkv():
        return mate_copy(10, dkv, dkv_mate)

    pl.semaphore_wait(barrier, len(peers))
    for kv in range(2):
        for which in range(2):
            for n in range(2):
                kv_copy(kv, n, which).start()

    load(4).wait()

    def transpose(n, carry):
        cols = pl.ds(pl.multiple_of(n * 256, 256), 256)
        xt[cols, :] = x_nat[:, cols].T
        return carry

    lax.fori_loop(0, D // 256, transpose, 0)
    for j in range(8):
        mate_x(j).start()

    first_row = seq * ROWS
    dk_acc[...] = jnp.zeros_like(dk_acc)
    dv_acc[...] = jnp.zeros_like(dv_acc)

    def make_bias(b, carry):
        bias[b] = row_bias(lengths, first_row, b * BLOCK)
        return carry

    lax.fori_loop(0, ROWS // BLOCK, make_bias, 0)
    for n in range(4):
        load(n).wait()

    def attend(kv, b):
        i0 = pl.multiple_of(b * BLOCK, BLOCK)
        rows, span = pl.ds(i0, BLOCK), pl.ds(i0, SPAN)
        lanes = slice(kv * HD, (kv + 1) * HD)
        heads = [slice(n * HD, (n + 1) * HD) for n in (2 * kv, 2 * kv + 1)]
        q2 = jnp.concatenate([q[rows, h] for h in heads], axis=0)
        g2 = jnp.concatenate([g[rows, h] for h in heads], axis=0)
        k, v = keys[span, lanes], values[span, lanes]
        both = jnp.concatenate([bias[b], bias[b]], axis=0)
        scores = dot(q2, k, NT) + both
        top = jnp.max(scores, axis=1, keepdims=True)
        weight = jnp.exp2((scores - top) * EXP2_SCALE)
        probs = weight * (1.0 / jnp.sum(weight, axis=1, keepdims=True))
        low = probs.astype(BF16)
        prob_grad = dot(g2, v, NT)
        delta = jnp.sum(low.astype(F32) * prob_grad, axis=1, keepdims=True)
        score_low = (probs * (prob_grad - delta)).astype(BF16)
        query_grad = (dot(score_low, k, NN) * SCALE).astype(BF16)
        dq[rows, heads[0]] = query_grad[:BLOCK]
        dq[rows, heads[1]] = query_grad[BLOCK:]
        dk_acc[kv, :, span] += dot(q2.T, score_low, NN)
        dv_acc[kv, :, span] += dot(g2.T, low, NN)

    for kv in range(2):
        for which in range(2):
            for n in range(2):
                kv_copy(kv, n, which).wait_recv()

        def pair(b, carry, kv=kv):
            attend(kv, 2 * b)
            attend(kv, 2 * b + 1)
            return carry

        lax.fori_loop(0, ROWS // BLOCK // 2, pair, 0)
        for n in (1, 0):
            cols = slice(WINDOW - (n + 1) * ROWS, WINDOW - n * ROWS)
            halo_out[kv, n, 0] = (dk_acc[kv, :, cols] * SCALE).astype(BF16)
            halo_out[kv, n, 1] = dv_acc[kv, :, cols].astype(BF16)
            for which in range(2):
                grad_copy(kv, n, which).start()
        mate_dq(kv).start()

    def hop(axis, unit, n, src, dst, device):
        return remote(src, dst, send_sem.at[axis, unit, n], recv_sem.at[axis, unit, n], device)

    def opposite(axis, unit, way):
        device = (right, left)[way][axis]
        rows = WAY_ROWS[way]
        return hop(axis, unit, way, part.at[axis, unit, 0, rows], relay.at[axis, unit, rows], device)

    def plain(axis, unit, way):
        device = (right, left)[way][axis]
        rows = WAY_ROWS[1 - way]
        return hop(
            axis, unit, 2 + way, part.at[axis, unit, 1 + way, rows], final.at[axis, unit, way, rows], device
        )

    def summed(axis, unit, way):
        device = (right, left)[way][axis]
        rows = WAY_ROWS[way]
        return hop(
            axis, unit, 4 + way, part.at[axis, unit, 1 + way, rows], final.at[axis, unit, way, rows], device
        )

    def crossing(axis, unit, way):
        rows = WAY_ROWS[way]
        slot = unit // 2 if axis == WEIGHT else unit
        src = part.at[axis, unit, 3, rows]
        if axis == WEIGHT:
            return hop(axis, unit, 6 + way, src, zrelay.at[slot, rows], (above, below)[way])
        return hop(axis, unit, 6 + way, src, zland.at[axis, slot, rows], beside)

    def onward(unit, way):
        rows = WAY_ROWS[way]
        slot = unit // 2
        return hop(
            WEIGHT, unit, 8 + way, zrelay.at[slot, rows], zland.at[WEIGHT, slot, rows], (above, below)[way]
        )

    def target(axis, side, u):
        off = 2 - u + (u // 2) * 3 - (u // 3) * 2
        z = (1 - depth[axis] + side) % 2
        return z * 4 + (place[axis] + off) % 4

    def make_weight(unit):
        side, half = unit % 2, unit // 2
        own, other, dims = ((dq, dq_mate, NN), (dkv, dkv_mate, NT))[half]

        def body(u, carry):
            j = target(WEIGHT, side, u)
            product = dot(xt[block_rows(2 * j + core), :], own[...], dims)
            product += dot(x_mate[j], other[...], dims)
            part[WEIGHT, unit, u] = product.astype(BF16)
            return carry

        lax.fori_loop(0, 4, body, 0)

    def make_input(unit):
        side, half = unit // 2, unit % 2

        def body(u, carry):
            j = target(INPUT, side, u) * 2 + half
            product = dot(wq[j], dq[...], NT)
            product += dot(wkv[j], dkv[...], NN)
            part[INPUT, unit, u] = product.astype(BF16)
            return carry

        lax.fori_loop(0, 4, body, 0)

    def send(axis, unit):
        for way in range(2):
            opposite(axis, unit, way).start()
        for way in range(2):
            plain(axis, unit, way).start()

    def forward(axis, unit):
        for way in range(2):
            opposite(axis, unit, way).wait_recv()
            rows = WAY_ROWS[way]
            kept = part[axis, unit, 1 + way, rows].astype(F32)
            part[axis, unit, 1 + way, rows] = (kept + relay[axis, unit, rows].astype(F32)).astype(BF16)
            summed(axis, unit, way).start()

    def collected(axis, unit):
        for way in range(2):
            plain(axis, unit, way).wait_recv()
            summed(axis, unit, way).wait_recv()
        total = part[axis, unit, 3].astype(F32)
        return total + final[axis, unit, 0].astype(F32) + final[axis, unit, 1].astype(F32)

    def cross(axis, unit):
        part[axis, unit, 3] = collected(axis, unit).astype(BF16)
        for way in range(2):
            crossing(axis, unit, way).start()

    def carry_on(unit):
        for way in range(2):
            crossing(WEIGHT, unit, way).wait_recv()
            onward(unit, way).start()

    def finished(axis, unit):
        total = collected(axis, unit)
        source = unit - 1 if axis == WEIGHT else unit - 2
        slot = source // 2 if axis == WEIGHT else source
        for way in range(2):
            if axis == WEIGHT:
                onward(source, way).wait_recv()
            else:
                crossing(axis, source, way).wait_recv()
        return (total + zland[axis, slot].astype(F32)).astype(BF16)

    for j in range(8):
        mate_x(j).wait_recv()
    for kv in range(2):
        mate_dq(kv).wait_recv()
    make_weight(0)
    send(WEIGHT, 0)
    make_weight(1)
    forward(WEIGHT, 0)
    send(WEIGHT, 1)

    for kv in range(2):
        for n in range(2):
            for which in range(2):
                grad_copy(kv, n, which).wait_recv()
        own = slice(WINDOW, EXT)
        halo = [halo_in[kv, 0, n].astype(F32) + halo_in[kv, 1, n].astype(F32) for n in range(2)]
        dkv[kv * HD:(kv + 1) * HD, :] = (dk_acc[kv, :, own] * SCALE + halo[0]).astype(BF16)
        dkv[(2 + kv) * HD:(3 + kv) * HD, :] = (dv_acc[kv, :, own] + halo[1]).astype(BF16)
    mate_dkv().start()
    for n in (5, 6, 7):
        load(n).wait()

    make_input(0)
    send(INPUT, 0)
    make_input(1)
    forward(WEIGHT, 1)
    forward(INPUT, 0)
    send(INPUT, 1)
    mate_dkv().wait_recv()
    make_weight(2)
    send(WEIGHT, 2)
    make_input(2)
    cross(WEIGHT, 0)
    forward(INPUT, 1)
    send(INPUT, 2)
    make_weight(3)
    forward(WEIGHT, 2)
    send(WEIGHT, 3)
    make_input(3)
    carry_on(0)
    cross(INPUT, 0)
    forward(INPUT, 2)
    send(INPUT, 3)
    forward(WEIGHT, 3)
    cross(WEIGHT, 2)
    cross(INPUT, 1)
    carry_on(2)
    forward(INPUT, 3)
    out_q[...] = finished(WEIGHT, 1)
    out_kv[...] = finished(WEIGHT, 3)
    out_h[:PIECE, :] = finished(INPUT, 2)
    out_h[PIECE:, :] = finished(INPUT, 3)

    for kv in range(2):
        mate_dq(kv).wait_send()
        for n in range(2):
            for which in range(2):
                kv_copy(kv, n, which).wait_send()
                grad_copy(kv, n, which).wait_send()
    for j in range(8):
        mate_x(j).wait_send()
    mate_dkv().wait_send()
    for axis in range(2):
        for unit in range(4):
            for way in range(2):
                opposite(axis, unit, way).wait_send()
                plain(axis, unit, way).wait_send()
                summed(axis, unit, way).wait_send()
                if axis == WEIGHT and unit % 2 == 0:
                    crossing(axis, unit, way).wait_send()
                    onward(unit, way).wait_send()
                if axis == INPUT and unit < 2:
                    crossing(axis, unit, way).wait_send()


def whole_step(lengths, x, q, g, k, v, wq, wk, wv):
    vmem = pl.BlockSpec(memory_space=pltpu.VMEM)
    anywhere = pl.BlockSpec(memory_space=pl.ANY)
    dma = pltpu.SemaphoreType.DMA
    piece = (PIECE, COLS)
    return pl.pallas_call(
        step_kernel,
        out_shape=[
            jax.ShapeDtypeStruct((2 * PIECE, ROWS), BF16),
            jax.ShapeDtypeStruct(piece, BF16),
            jax.ShapeDtypeStruct(piece, BF16),
        ],
        in_specs=[pl.BlockSpec(memory_space=pltpu.SMEM)] + [anywhere] * 8,
        out_specs=[vmem] * 3,
        scratch_shapes=[
            pltpu.VMEM((ROWS, D), BF16),
            pltpu.VMEM((D, ROWS), BF16),
            pltpu.VMEM((8, PIECE, ROWS), BF16),
            pltpu.VMEM((ROWS, COLS), BF16),
            pltpu.VMEM((ROWS, COLS), BF16),
            pltpu.VMEM((EXT, 2 * HD), BF16),
            pltpu.VMEM((EXT, 2 * HD), BF16),
            pltpu.VMEM((16, PIECE, COLS), BF16),
            pltpu.VMEM((16, PIECE, COLS), BF16),
            pltpu.VMEM((ROWS // BLOCK, BLOCK, SPAN), F32),
            pltpu.VMEM((2, HD, EXT), F32),
            pltpu.VMEM((2, HD, EXT), F32),
            pltpu.VMEM((ROWS, COLS), BF16),
            pltpu.VMEM((ROWS, COLS), BF16),
            pltpu.VMEM((COLS, ROWS), BF16),
            pltpu.VMEM((COLS, ROWS), BF16),
            pltpu.VMEM((2, 2, 2, HD, ROWS), BF16),
            pltpu.VMEM((2, 2, 2, HD, ROWS), BF16),
            pltpu.VMEM((2, 4, 4) + piece, BF16),
            pltpu.VMEM((2, 4) + piece, BF16),
            pltpu.VMEM((2, 4, 2) + piece, BF16),
            pltpu.VMEM((2, 2) + piece, BF16),
            pltpu.VMEM((2,) + piece, BF16),
            dma((8,)),
            dma((2, 2, 2)),
            dma((2, 2, 2)),
            dma((2, 2, 2)),
            dma((2, 2, 2)),
            dma((11,)),
            dma((11,)),
            dma((2, 4, 10)),
            dma((2, 4, 10)),
        ],
        compiler_params=pltpu.CompilerParams(
            collective_id=1, has_side_effects=True, vmem_limit_bytes=67043328
        ),
        name="step",
    )(lengths, x, q, g, k, v, wq, wk, wv)


def write_kernel(h, q, kv, out_h, out_q, out_k, out_v):
    out_h[...] = h[...].T
    out_q[...] = q[...]
    out_k[...] = kv[:, : 2 * HD]
    out_v[...] = kv[:, 2 * HD:]


def written(h, q, kv):
    vmem = pl.BlockSpec(memory_space=pltpu.VMEM)
    shapes = ((ROWS, 2 * PIECE), (PIECE, COLS), (PIECE, COLS // 2), (PIECE, COLS // 2))
    return pl.pallas_call(
        write_kernel,
        out_shape=[jax.ShapeDtypeStruct(shape, BF16) for shape in shapes],
        in_specs=[vmem] * 3,
        out_specs=[vmem] * 4,
        name="write",
    )(h, q, kv)


def on_device(layer_input, query, keys, values, out_grad, w_query, w_key, w_value, proof_lengths):
    weights = [w.reshape(16, PIECE, -1) for w in (w_query, w_key, w_value)]
    return tuple(written(*whole_step(proof_lengths, layer_input, query, out_grad, keys, values, *weights)))


def solution(mesh):
    return jax.shard_map(
        on_device,
        mesh=mesh,
        in_specs=(
            P("seq", None),
            P("seq", "head"),
            P("seq", "head"),
            P("seq", "head"),
            P("seq", "head"),
            P(None, "head"),
            P(None, "head"),
            P(None, "head"),
            P(),
        ),
        out_specs=(P("seq", "head"), P("seq", "head"), P("seq", "head"), P("seq", "head")),
        check_vma=False,
    )
```

```python
import math

import jax
import jax.numpy as jnp
from jax import lax
from jax.experimental import pallas as pl
from jax.experimental.pallas import tpu as pltpu
from jax.sharding import PartitionSpec as P

D = 5376
H = 32
HD = 128
WINDOW = 1024
ROWS = 512
BLOCK = 128
SPAN = WINDOW + BLOCK
EXT = WINDOW + ROWS
SCALE = (D // H) ** -0.5
EXP2_SCALE = SCALE * math.log2(math.e)
F32 = jnp.float32
BF16 = jnp.bfloat16
PIECE = 336
CUT = 176
COLS = 512
MESH = pl.DeviceIdType.MESH

NN = (((1,), (0,)), ((), ()))
NT = (((1,), (1,)), ((), ()))

WEIGHT, INPUT = 0, 1
WAY_ROWS = (slice(0, CUT), slice(CUT, PIECE))


def dot(left, right, dims):
    return lax.dot_general(left, right, dims, preferred_element_type=F32)


def row_bias(lengths, first_row, i0):
    row = lax.broadcasted_iota(jnp.int32, (BLOCK, 1), 0)
    position = first_row + i0 + row
    start = jnp.zeros((BLOCK, 1), jnp.int32)
    proof_start = jnp.int32(0)
    for proof in range(lengths.shape[0]):
        start = jnp.maximum(start, jnp.where(position >= proof_start, proof_start, 0))
        proof_start = proof_start + lengths[proof]
    lowest = jnp.maximum(start, position - (WINDOW - 1))
    lowest = lowest - (first_row - WINDOW) - i0
    column = lax.broadcasted_iota(jnp.int32, (BLOCK, SPAN), 1)
    seen = (column >= lowest) & (column <= row + WINDOW)
    return jnp.where(seen, 0.0, -1e30).astype(F32)


def step_kernel(
    lengths, x, q_in, g_in, k_in, v_in, wq_in, wk_in, wv_in,
    out_h, out_q, out_kv,
    x_nat, xt, x_mate, q, g, keys, values, wq, wkv, bias, dk_acc, dv_acc,
    dq, dq_mate, dkv, dkv_mate, halo_out, halo_in, mate_far,
    part, relay, final, zland,
    load_sem, kv_send, kv_recv, gh_send, gh_recv, mate_send, mate_recv,
    send_sem, recv_sem,
):
    seq = lax.axis_index("seq")
    head = lax.axis_index("head")
    core, px, zh = seq % 2, (seq // 2) % 4, seq // 8
    py, zl = head % 4, head // 4
    zz = zh * 2 + zl

    def at(z_, x_, core_, y_):
        return {"seq": (z_ // 2) * 8 + x_ * 2 + core_, "head": (z_ % 2) * 4 + y_}

    far_z = (zz + 2) % 4
    next_z, prev_z = (zz + 2 * (px // 3)) % 4, (zz + 2 * ((3 - px) // 3)) % 4
    chip = zh * 4 + px
    mate = at(zz, px, 1 - core, py)
    right = (at(zz, (px + 1) % 4, core, py), at(zz, px, core, (py + 1) % 4))
    left = (at(zz, (px + 3) % 4, core, py), at(zz, px, core, (py + 3) % 4))
    across = (at(far_z, px, core, py), at(zh * 2 + 1 - zl, px, core, py))
    place, depth = (px, py), (zh, zl)

    barrier = pltpu.get_barrier_semaphore()
    peers = [mate, right[1], left[1], across[0], across[1]]
    for k in range(2):
        peers += [at(zz, (px + 1) % 4, k, py), at(zz, (px + 3) % 4, k, py), at(far_z, 3 - px, k, py)]
    for peer in peers:
        pl.semaphore_signal(barrier, inc=1, device_id=peer, device_id_type=MESH)

    places = (
        (q_in, q),
        (g_in, g),
        (k_in, keys.at[WINDOW:EXT, :]),
        (v_in, values.at[WINDOW:EXT, :]),
        (x, x_nat),
        (wq_in, wq),
        (wk_in, wkv.at[:, :, : 2 * HD]),
        (wv_in, wkv.at[:, :, 2 * HD:]),
    )

    def load(n):
        return pltpu.make_async_copy(*places[n], load_sem.at[n])

    for n in range(5):
        load(n).start()

    def remote(src, dst, send, recv, device):
        return pltpu.make_async_remote_copy(
            src_ref=src, dst_ref=dst, send_sem=send, recv_sem=recv,
            device_id=device, device_id_type=MESH,
        )

    def head_lanes(kv):
        return slice(kv * HD, (kv + 1) * HD)

    def kv_remote(kv, slot, which, src, rows, send, device):
        dst = (keys, values)[which].at[rows, head_lanes(kv)]
        return remote(src, dst, kv_send.at[kv, send, which], kv_recv.at[kv, slot, which], device)

    def kv_source(kv, which):
        return (k_in, v_in)[which].at[:, head_lanes(kv)]

    core_rows = pl.ds(pl.multiple_of(core * ROWS, ROWS), ROWS)
    near, far = slice(ROWS, WINDOW), slice(0, ROWS)

    def kv_next(kv, which):
        device = at(next_z, (px + 1) % 4, 0, py)
        dst = (keys, values)[which].at[core_rows, head_lanes(kv)]
        return remote(
            kv_source(kv, which), dst, kv_send.at[kv, 0, which], kv_recv.at[kv, core, which], device
        )

    def kv_mate(kv, which):
        return kv_remote(kv, 1, which, kv_source(kv, which), near, 1, mate)

    def kv_share(kv, which):
        src = (keys, values)[which].at[near, head_lanes(kv)]
        return kv_remote(kv, 0, which, src, far, 2, mate)

    def kv_arrived(kv, slot, which):
        kv_remote(kv, slot, which, kv_source(kv, which), (far, near)[slot], 0, mate).wait_recv()

    def grad_mate(kv, n, which):
        dst = halo_in.at[kv, 0, which] if n == 0 else mate_far.at[kv, which]
        return remote(
            halo_out.at[kv, n, which], dst, gh_send.at[kv, n, which], gh_recv.at[kv, 2 * n, which], mate
        )

    def grad_prev(kv, n, which):
        device = at(prev_z, (px + 3) % 4, 1 - n, py)
        return remote(
            halo_out.at[kv, n, which], halo_in.at[kv, 1, which],
            gh_send.at[kv, n, which], gh_recv.at[kv, 1, which], device,
        )

    def mate_copy(n, src, dst):
        return remote(src, dst, mate_send.at[n], mate_recv.at[n], mate)

    def block_rows(index):
        return pl.ds(pl.multiple_of(index * PIECE, 16), PIECE)

    def mate_x(j):
        return mate_copy(j, xt.at[block_rows(2 * j + 1 - core), :], x_mate.at[j])

    def mate_dq(kv):
        lanes = slice(kv * 2 * HD, (kv + 1) * 2 * HD)
        return mate_copy(8 + kv, dq.at[:, lanes], dq_mate.at[:, lanes])

    def mate_dkv():
        return mate_copy(10, dkv, dkv_mate)

    first_core, second_core = core == 0, core == 1
    has_prev, has_next = chip > 0, chip < 7
    both = range(2)

    pl.semaphore_wait(barrier, len(peers))

    for kv in both:
        for which in both:
            @pl.when(has_next)
            def _():
                kv_next(kv, which).start()

            @pl.when(first_core)
            def _():
                kv_mate(kv, which).start()

    @pl.when(chip == 0)
    def _():
        keys[far, :] = jnp.zeros((ROWS, 2 * HD), BF16)
        values[far, :] = jnp.zeros((ROWS, 2 * HD), BF16)

    @pl.when(seq == 0)
    def _():
        keys[near, :] = jnp.zeros((ROWS, 2 * HD), BF16)
        values[near, :] = jnp.zeros((ROWS, 2 * HD), BF16)

    @pl.when(second_core)
    def _():
        halo_in[:, 0] = jnp.zeros((2, 2, HD, ROWS), BF16)

    @pl.when(chip == 7)
    def _():
        halo_in[:, 1] = jnp.zeros((2, 2, HD, ROWS), BF16)

    for n in (5, 6, 7):
        load(n).start()

    load(4).wait()

    def transpose(n, carry):
        cols = pl.ds(pl.multiple_of(n * 256, 256), 256)
        xt[cols, :] = x_nat[:, cols].T
        return carry

    lax.fori_loop(0, D // 256, transpose, 0)

    first_row = seq * ROWS
    dk_acc[...] = jnp.zeros_like(dk_acc)
    dv_acc[...] = jnp.zeros_like(dv_acc)

    def make_bias(b, carry):
        bias[b] = row_bias(lengths, first_row, b * BLOCK)
        return carry

    lax.fori_loop(0, ROWS // BLOCK, make_bias, 0)
    for n in range(4):
        load(n).wait()

    def attend(kv, b):
        i0 = pl.multiple_of(b * BLOCK, BLOCK)
        rows, span = pl.ds(i0, BLOCK), pl.ds(i0, SPAN)
        lanes = slice(kv * HD, (kv + 1) * HD)
        heads = [slice(n * HD, (n + 1) * HD) for n in (2 * kv, 2 * kv + 1)]
        q2 = jnp.concatenate([q[rows, h] for h in heads], axis=0)
        g2 = jnp.concatenate([g[rows, h] for h in heads], axis=0)
        k, v = keys[span, lanes], values[span, lanes]
        scores = dot(q2, k, NT) + jnp.concatenate([bias[b], bias[b]], axis=0)
        top = jnp.max(scores, axis=1, keepdims=True)
        weight = jnp.exp2((scores - top) * EXP2_SCALE)
        probs = weight * (1.0 / jnp.sum(weight, axis=1, keepdims=True))
        low = probs.astype(BF16)
        prob_grad = dot(g2, v, NT)
        delta = jnp.sum(low.astype(F32) * prob_grad, axis=1, keepdims=True)
        score_low = (probs * (prob_grad - delta)).astype(BF16)
        query_grad = (dot(score_low, k, NN) * SCALE).astype(BF16)
        dq[rows, heads[0]] = query_grad[:BLOCK]
        dq[rows, heads[1]] = query_grad[BLOCK:]
        dk_acc[kv, :, span] += dot(q2.T, score_low, NN)
        dv_acc[kv, :, span] += dot(g2.T, low, NN)

    def kv_ready(kv):
        @pl.when(first_core & has_prev)
        def _():
            for which in both:
                kv_arrived(kv, 1, which)
                kv_share(kv, which).start()
            for which in both:
                kv_arrived(kv, 0, which)

        @pl.when(second_core)
        def _():
            for which in both:
                kv_arrived(kv, 1, which)

        @pl.when(second_core & has_prev)
        def _():
            for which in both:
                kv_arrived(kv, 0, which)

    def to_prev(kv, n):
        for which in both:
            grad_prev(kv, n, which).start()

    def grads_out(kv):
        for n in (1, 0):
            cols = slice(WINDOW - (n + 1) * ROWS, WINDOW - n * ROWS)
            halo_out[kv, n, 0] = (dk_acc[kv, :, cols] * SCALE).astype(BF16)
            halo_out[kv, n, 1] = dv_acc[kv, :, cols].astype(BF16)

            if n == 1:
                @pl.when(second_core & has_prev)
                def _():
                    for which in both:
                        grad_mate(kv, 1, which).start()

                @pl.when(first_core & has_prev)
                def _():
                    to_prev(kv, 1)
            else:
                @pl.when(second_core)
                def _():
                    for which in both:
                        grad_mate(kv, 0, which).start()

    def grads_joined(kv):
        @pl.when(first_core & has_prev)
        def _():
            for which in both:
                grad_mate(kv, 1, which).wait_recv()
                term = halo_out[kv, 0, which].astype(F32) + mate_far[kv, which].astype(F32)
                halo_out[kv, 0, which] = term.astype(BF16)
            to_prev(kv, 0)

    for kv in both:
        kv_ready(kv)
        if kv == 0:
            for j in range(8):
                mate_x(j).start()

        def pair(b, carry, kv=kv):
            if kv == 1:
                @pl.when(b == 1)
                def _():
                    grads_joined(0)

            attend(kv, 2 * b)
            attend(kv, 2 * b + 1)
            return carry

        lax.fori_loop(0, ROWS // BLOCK // 2, pair, 0)
        grads_out(kv)
        mate_dq(kv).start()
    grads_joined(1)

    def hop(axis, unit, n, src, dst, device):
        return remote(src, dst, send_sem.at[axis, unit, n], recv_sem.at[axis, unit, n], device)

    def opposite(axis, unit, way):
        device = (right, left)[way][axis]
        rows = WAY_ROWS[way]
        return hop(axis, unit, way, part.at[axis, unit, 0, rows], relay.at[axis, unit, rows], device)

    def plain(axis, unit, way):
        device = (right, left)[way][axis]
        rows = WAY_ROWS[1 - way]
        return hop(
            axis, unit, 2 + way, part.at[axis, unit, 1 + way, rows], final.at[axis, unit, way, rows], device
        )

    def summed(axis, unit, way):
        device = (right, left)[way][axis]
        rows = WAY_ROWS[way]
        return hop(
            axis, unit, 4 + way, part.at[axis, unit, 1 + way, rows], final.at[axis, unit, way, rows], device
        )

    def crossing(axis, unit, way):
        rows = WAY_ROWS[way]
        slot = unit // 2 if axis == WEIGHT else unit
        return hop(axis, unit, 6 + way, part.at[axis, unit, 3, rows], zland.at[axis, slot, rows], across[axis])

    def target(axis, side, u):
        off = 2 - u + (u // 2) * 3 - (u // 3) * 2
        z = (1 - depth[axis] + side) % 2
        return z * 4 + (place[axis] + off) % 4

    def eager(axis, unit, u):
        @pl.when(u == 0)
        def _():
            for way in both:
                opposite(axis, unit, way).start()

        for way in both:
            @pl.when(u == 1 + way)
            def _():
                plain(axis, unit, way).start()

    def make_weight(unit):
        side, half = unit % 2, unit // 2
        own, other, dims = ((dq, dq_mate, NN), (dkv, dkv_mate, NT))[half]

        def body(u, carry):
            j = target(WEIGHT, side, u)
            product = dot(xt[block_rows(2 * j + core), :], own[...], dims)
            product += dot(x_mate[j], other[...], dims)
            part[WEIGHT, unit, u] = product.astype(BF16)
            return carry

        lax.fori_loop(0, 4, body, 0)

    def make_input(unit):
        side, half = unit // 2, unit % 2

        def body(u, carry):
            j = target(INPUT, side, u) * 2 + half
            product = dot(wq[j], dq[...], NT)
            product += dot(wkv[j], dkv[...], NN)
            part[INPUT, unit, u] = product.astype(BF16)
            if unit == 0:
                eager(INPUT, unit, u)
            return carry

        lax.fori_loop(0, 4, body, 0)

    def send(axis, unit):
        for way in range(2):
            opposite(axis, unit, way).start()
        for way in range(2):
            plain(axis, unit, way).start()

    def forward(axis, unit):
        for way in range(2):
            opposite(axis, unit, way).wait_recv()
            rows = WAY_ROWS[way]
            kept = part[axis, unit, 1 + way, rows].astype(F32)
            part[axis, unit, 1 + way, rows] = (kept + relay[axis, unit, rows].astype(F32)).astype(BF16)
            summed(axis, unit, way).start()

    def collected(axis, unit):
        for way in range(2):
            plain(axis, unit, way).wait_recv()
            summed(axis, unit, way).wait_recv()
        total = part[axis, unit, 3].astype(F32)
        return total + final[axis, unit, 0].astype(F32) + final[axis, unit, 1].astype(F32)

    def cross(axis, unit):
        part[axis, unit, 3] = collected(axis, unit).astype(BF16)
        for way in range(2):
            crossing(axis, unit, way).start()

    def finished(axis, unit):
        total = collected(axis, unit)
        source = unit - 1 if axis == WEIGHT else unit - 2
        slot = source // 2 if axis == WEIGHT else source
        for way in range(2):
            crossing(axis, source, way).wait_recv()
        return (total + zland[axis, slot].astype(F32)).astype(BF16)

    for j in range(8):
        mate_x(j).wait_recv()
    for kv in range(2):
        mate_dq(kv).wait_recv()
    make_weight(0)
    opposite(WEIGHT, 0, 0).start()
    plain(WEIGHT, 0, 0).start()
    make_weight(1)

    own = slice(WINDOW, EXT)
    for kv in both:
        for which in both:
            @pl.when(first_core)
            def _():
                grad_mate(kv, 0, which).wait_recv()

            @pl.when(has_next)
            def _():
                grad_prev(kv, 0, which).wait_recv()

        halo = [halo_in[kv, 0, n].astype(F32) + halo_in[kv, 1, n].astype(F32) for n in both]
        dkv[kv * HD:(kv + 1) * HD, :] = (dk_acc[kv, :, own] * SCALE + halo[0]).astype(BF16)
        dkv[(2 + kv) * HD:(3 + kv) * HD, :] = (dv_acc[kv, :, own] + halo[1]).astype(BF16)
    mate_dkv().start()
    for n in (5, 6, 7):
        load(n).wait()

    make_input(0)
    opposite(WEIGHT, 0, 1).start()
    plain(WEIGHT, 0, 1).start()
    make_input(1)
    mate_dkv().wait_recv()
    make_weight(2)
    forward(INPUT, 0)
    send(INPUT, 1)
    forward(WEIGHT, 0)
    send(WEIGHT, 1)
    make_input(2)
    make_weight(3)
    make_input(3)
    cross(INPUT, 0)
    cross(WEIGHT, 0)
    forward(INPUT, 1)
    send(INPUT, 2)
    forward(WEIGHT, 1)
    send(WEIGHT, 2)
    cross(INPUT, 1)
    forward(INPUT, 2)
    send(INPUT, 3)
    forward(WEIGHT, 2)
    send(WEIGHT, 3)
    cross(WEIGHT, 2)
    out_q[...] = finished(WEIGHT, 1)
    forward(INPUT, 3)
    forward(WEIGHT, 3)
    out_h[:PIECE, :] = finished(INPUT, 2)
    out_h[PIECE:, :] = finished(INPUT, 3)
    out_kv[...] = finished(WEIGHT, 3)

    for kv in both:
        mate_dq(kv).wait_send()
        for which in both:
            @pl.when(has_next)
            def _():
                kv_next(kv, which).wait_send()

            @pl.when(first_core)
            def _():
                kv_mate(kv, which).wait_send()

            @pl.when(first_core & has_prev)
            def _():
                kv_share(kv, which).wait_send()

            @pl.when(second_core)
            def _():
                grad_mate(kv, 0, which).wait_send()

            @pl.when(second_core & has_prev)
            def _():
                grad_mate(kv, 1, which).wait_send()

            @pl.when(first_core & has_prev)
            def _():
                grad_prev(kv, 0, which).wait_send()
                grad_prev(kv, 1, which).wait_send()

    for j in range(8):
        mate_x(j).wait_send()
    mate_dkv().wait_send()
    for axis in range(2):
        for unit in range(4):
            for way in range(2):
                opposite(axis, unit, way).wait_send()
                plain(axis, unit, way).wait_send()
                summed(axis, unit, way).wait_send()
                if axis == WEIGHT and unit % 2 == 0:
                    crossing(axis, unit, way).wait_send()
                if axis == INPUT and unit < 2:
                    crossing(axis, unit, way).wait_send()


def whole_step(lengths, x, q, g, k, v, wq, wk, wv):
    vmem = pl.BlockSpec(memory_space=pltpu.VMEM)
    anywhere = pl.BlockSpec(memory_space=pl.ANY)
    dma = pltpu.SemaphoreType.DMA
    piece = (PIECE, COLS)
    return pl.pallas_call(
        step_kernel,
        out_shape=[
            jax.ShapeDtypeStruct((2 * PIECE, ROWS), BF16),
            jax.ShapeDtypeStruct(piece, BF16),
            jax.ShapeDtypeStruct(piece, BF16),
        ],
        in_specs=[pl.BlockSpec(memory_space=pltpu.SMEM)] + [anywhere] * 8,
        out_specs=[vmem] * 3,
        scratch_shapes=[
            pltpu.VMEM((ROWS, D), BF16),
            pltpu.VMEM((D, ROWS), BF16),
            pltpu.VMEM((8, PIECE, ROWS), BF16),
            pltpu.VMEM((ROWS, COLS), BF16),
            pltpu.VMEM((ROWS, COLS), BF16),
            pltpu.VMEM((EXT, 2 * HD), BF16),
            pltpu.VMEM((EXT, 2 * HD), BF16),
            pltpu.VMEM((16, PIECE, COLS), BF16),
            pltpu.VMEM((16, PIECE, COLS), BF16),
            pltpu.VMEM((ROWS // BLOCK, BLOCK, SPAN), F32),
            pltpu.VMEM((2, HD, EXT), F32),
            pltpu.VMEM((2, HD, EXT), F32),
            pltpu.VMEM((ROWS, COLS), BF16),
            pltpu.VMEM((ROWS, COLS), BF16),
            pltpu.VMEM((COLS, ROWS), BF16),
            pltpu.VMEM((COLS, ROWS), BF16),
            pltpu.VMEM((2, 2, 2, HD, ROWS), BF16),
            pltpu.VMEM((2, 2, 2, HD, ROWS), BF16),
            pltpu.VMEM((2, 2, HD, ROWS), BF16),
            pltpu.VMEM((2, 4, 4) + piece, BF16),
            pltpu.VMEM((2, 4) + piece, BF16),
            pltpu.VMEM((2, 4, 2) + piece, BF16),
            pltpu.VMEM((2, 2) + piece, BF16),
            dma((8,)),
            dma((2, 3, 2)),
            dma((2, 2, 2)),
            dma((2, 2, 2)),
            dma((2, 3, 2)),
            dma((11,)),
            dma((11,)),
            dma((2, 4, 8)),
            dma((2, 4, 8)),
        ],
        compiler_params=pltpu.CompilerParams(
            collective_id=1, has_side_effects=True, vmem_limit_bytes=67043328
        ),
        name="step",
    )(lengths, x, q, g, k, v, wq, wk, wv)


def write_kernel(h, q, kv, out_h, out_q, out_k, out_v):
    out_h[...] = h[...]
    out_q[...] = q[...]
    out_k[...] = kv[:, : 2 * HD]
    out_v[...] = kv[:, 2 * HD:]


def written(h, q, kv):
    vmem = pl.BlockSpec(memory_space=pltpu.VMEM)
    shapes = ((2 * PIECE, ROWS), (PIECE, COLS), (PIECE, COLS // 2), (PIECE, COLS // 2))
    return pl.pallas_call(
        write_kernel,
        out_shape=[jax.ShapeDtypeStruct(shape, BF16) for shape in shapes],
        in_specs=[vmem] * 3,
        out_specs=[vmem] * 4,
        name="write",
    )(h, q, kv)


def on_device(layer_input, query, keys, values, out_grad, w_query, w_key, w_value, proof_lengths):
    weights = [w.reshape(16, PIECE, -1) for w in (w_query, w_key, w_value)]
    results = whole_step(proof_lengths, layer_input, query, out_grad, keys, values, *weights)
    input_grad, wq_grad, wk_grad, wv_grad = written(*results)
    return (input_grad.T, wq_grad, wk_grad, wv_grad)


def solution(mesh):
    return jax.shard_map(
        on_device,
        mesh=mesh,
        in_specs=(
            P("seq", None),
            P("seq", "head"),
            P("seq", "head"),
            P("seq", "head"),
            P("seq", "head"),
            P(None, "head"),
            P(None, "head"),
            P(None, "head"),
            P(),
        ),
        out_specs=(P("seq", "head"), P("seq", "head"), P("seq", "head"), P("seq", "head")),
        check_vma=False,
    )
```

```python
import math

import jax
import jax.numpy as jnp
from jax import lax
from jax.experimental import pallas as pl
from jax.experimental.pallas import tpu as pltpu
from jax.sharding import PartitionSpec as P

D = 5376
H = 32
HD = 128
WINDOW = 1024
ROWS = 512
BLOCK = 128
SPAN = WINDOW + BLOCK
EXT = WINDOW + ROWS
SCALE = (D // H) ** -0.5
EXP2_SCALE = SCALE * math.log2(math.e)
F32 = jnp.float32
BF16 = jnp.bfloat16
PIECE = 336
CUTS = (176, 176)
COLS = 512
MESH = pl.DeviceIdType.MESH

NN = (((1,), (0,)), ((), ()))
NT = (((1,), (1,)), ((), ()))

WEIGHT, INPUT = 0, 1
WAY_ROWS = [(slice(0, cut), slice(cut, PIECE)) for cut in CUTS]
HALF = COLS // 2


def dot(left, right, dims):
    return lax.dot_general(left, right, dims, preferred_element_type=F32)


def row_bias(lengths, first_row, i0):
    row = lax.broadcasted_iota(jnp.int32, (BLOCK, 1), 0)
    position = first_row + i0 + row
    start = jnp.zeros((BLOCK, 1), jnp.int32)
    proof_start = jnp.int32(0)
    for proof in range(lengths.shape[0]):
        start = jnp.maximum(start, jnp.where(position >= proof_start, proof_start, 0))
        proof_start = proof_start + lengths[proof]
    lowest = jnp.maximum(start, position - (WINDOW - 1))
    lowest = lowest - (first_row - WINDOW) - i0
    column = lax.broadcasted_iota(jnp.int32, (BLOCK, SPAN), 1)
    seen = (column >= lowest) & (column <= row + WINDOW)
    return jnp.where(seen, 0.0, -1e30).astype(F32)


def step_kernel(
    lengths, x, q_in, g_in, k_in, v_in, wq_in, wk_in, wv_in,
    out_h, out_q, out_kv,
    x_nat, xt, x_mate, q, g, keys, values, wq, wkv, bias, dk_acc, dv_acc,
    dq, dq_mate, dkv, dkv_mate, halo_out, halo_in, mate_far,
    part, relay, final, zland, zfirst,
    load_sem, kv_send, kv_recv, gh_send, gh_recv, mate_send, mate_recv,
    send_sem, recv_sem, early_send, early_recv,
):
    seq = lax.axis_index("seq")
    head = lax.axis_index("head")
    core, px, zh = seq % 2, (seq // 2) % 4, seq // 8
    py, zl = head % 4, head // 4
    zz = zh * 2 + zl

    def at(z_, x_, core_, y_):
        return {"seq": (z_ // 2) * 8 + x_ * 2 + core_, "head": (z_ % 2) * 4 + y_}

    far_z = (zz + 2) % 4
    next_z, prev_z = (zz + 2 * (px // 3)) % 4, (zz + 2 * ((3 - px) // 3)) % 4
    chip = zh * 4 + px
    mate = at(zz, px, 1 - core, py)
    right = (at(zz, (px + 1) % 4, core, py), at(zz, px, core, (py + 1) % 4))
    left = (at(zz, (px + 3) % 4, core, py), at(zz, px, core, (py + 3) % 4))
    across = (at(far_z, px, core, py), at(zh * 2 + 1 - zl, px, core, py))
    place, depth = (px, py), (zh, zl)

    barrier = pltpu.get_barrier_semaphore()
    peers = [mate, right[1], left[1], across[0], across[1]]
    for k in range(2):
        peers += [at(zz, (px + 1) % 4, k, py), at(zz, (px + 3) % 4, k, py), at(far_z, 3 - px, k, py)]
    for peer in peers:
        pl.semaphore_signal(barrier, inc=1, device_id=peer, device_id_type=MESH)

    places = (
        (q_in, q),
        (g_in, g),
        (k_in, keys.at[WINDOW:EXT, :]),
        (v_in, values.at[WINDOW:EXT, :]),
        (x, x_nat),
        (wq_in, wq),
        (wk_in, wkv.at[:, :, : 2 * HD]),
        (wv_in, wkv.at[:, :, 2 * HD:]),
    )

    def load(n):
        return pltpu.make_async_copy(*places[n], load_sem.at[n])

    for n in range(5):
        load(n).start()

    def remote(src, dst, send, recv, device):
        return pltpu.make_async_remote_copy(
            src_ref=src, dst_ref=dst, send_sem=send, recv_sem=recv,
            device_id=device, device_id_type=MESH,
        )

    def head_lanes(kv):
        return slice(kv * HD, (kv + 1) * HD)

    def kv_remote(kv, slot, which, src, rows, send, device):
        dst = (keys, values)[which].at[rows, head_lanes(kv)]
        return remote(src, dst, kv_send.at[kv, send, which], kv_recv.at[kv, slot, which], device)

    def kv_source(kv, which):
        return (k_in, v_in)[which].at[:, head_lanes(kv)]

    core_rows = pl.ds(pl.multiple_of(core * ROWS, ROWS), ROWS)
    near, far = slice(ROWS, WINDOW), slice(0, ROWS)

    def kv_next(kv, which):
        device = at(next_z, (px + 1) % 4, 0, py)
        dst = (keys, values)[which].at[core_rows, head_lanes(kv)]
        return remote(
            kv_source(kv, which), dst, kv_send.at[kv, 0, which], kv_recv.at[kv, core, which], device
        )

    def kv_mate(kv, which):
        return kv_remote(kv, 1, which, kv_source(kv, which), near, 1, mate)

    def kv_share(kv, which):
        src = (keys, values)[which].at[near, head_lanes(kv)]
        return kv_remote(kv, 0, which, src, far, 2, mate)

    def kv_arrived(kv, slot, which):
        kv_remote(kv, slot, which, kv_source(kv, which), (far, near)[slot], 0, mate).wait_recv()

    def grad_mate(kv, n, which):
        dst = halo_in.at[kv, 0, which] if n == 0 else mate_far.at[kv, which]
        return remote(
            halo_out.at[kv, n, which], dst, gh_send.at[kv, n, which], gh_recv.at[kv, 2 * n, which], mate
        )

    def grad_prev(kv, n, which):
        device = at(prev_z, (px + 3) % 4, 1 - n, py)
        return remote(
            halo_out.at[kv, n, which], halo_in.at[kv, 1, which],
            gh_send.at[kv, n, which], gh_recv.at[kv, 1, which], device,
        )

    def mate_copy(n, src, dst):
        return remote(src, dst, mate_send.at[n], mate_recv.at[n], mate)

    def block_rows(index):
        return pl.ds(pl.multiple_of(index * PIECE, 16), PIECE)

    def mate_x(j):
        return mate_copy(j, xt.at[block_rows(2 * j + 1 - core), :], x_mate.at[j])

    def mate_dq(kv):
        lanes = slice(kv * 2 * HD, (kv + 1) * 2 * HD)
        return mate_copy(8 + kv, dq.at[:, lanes], dq_mate.at[:, lanes])

    def mate_dkv():
        return mate_copy(10, dkv, dkv_mate)

    first_core, second_core = core == 0, core == 1
    has_prev, has_next = chip > 0, chip < 7
    both = range(2)

    pl.semaphore_wait(barrier, len(peers))

    for kv in both:
        for which in both:
            @pl.when(has_next)
            def _():
                kv_next(kv, which).start()

            @pl.when(first_core)
            def _():
                kv_mate(kv, which).start()

    @pl.when(chip == 0)
    def _():
        keys[far, :] = jnp.zeros((ROWS, 2 * HD), BF16)
        values[far, :] = jnp.zeros((ROWS, 2 * HD), BF16)

    @pl.when(seq == 0)
    def _():
        keys[near, :] = jnp.zeros((ROWS, 2 * HD), BF16)
        values[near, :] = jnp.zeros((ROWS, 2 * HD), BF16)

    @pl.when(second_core)
    def _():
        halo_in[:, 0] = jnp.zeros((2, 2, HD, ROWS), BF16)

    @pl.when(chip == 7)
    def _():
        halo_in[:, 1] = jnp.zeros((2, 2, HD, ROWS), BF16)

    for n in (5, 6, 7):
        load(n).start()

    load(4).wait()

    def transpose(n, carry):
        cols = pl.ds(pl.multiple_of(n * 256, 256), 256)
        xt[cols, :] = x_nat[:, cols].T
        return carry

    lax.fori_loop(0, D // 256, transpose, 0)

    first_row = seq * ROWS
    dk_acc[...] = jnp.zeros_like(dk_acc)
    dv_acc[...] = jnp.zeros_like(dv_acc)

    def make_bias(b, carry):
        bias[b] = row_bias(lengths, first_row, b * BLOCK)
        return carry

    lax.fori_loop(0, ROWS // BLOCK, make_bias, 0)
    for n in range(4):
        load(n).wait()

    def attend(kv, b):
        i0 = pl.multiple_of(b * BLOCK, BLOCK)
        rows, span = pl.ds(i0, BLOCK), pl.ds(i0, SPAN)
        lanes = slice(kv * HD, (kv + 1) * HD)
        heads = [slice(n * HD, (n + 1) * HD) for n in (2 * kv, 2 * kv + 1)]
        q2 = jnp.concatenate([q[rows, h] for h in heads], axis=0)
        g2 = jnp.concatenate([g[rows, h] for h in heads], axis=0)
        k, v = keys[span, lanes], values[span, lanes]
        scores = dot(q2, k, NT) + jnp.concatenate([bias[b], bias[b]], axis=0)
        top = jnp.max(scores, axis=1, keepdims=True)
        weight = jnp.exp2((scores - top) * EXP2_SCALE)
        probs = weight * (1.0 / jnp.sum(weight, axis=1, keepdims=True))
        low = probs.astype(BF16)
        prob_grad = dot(g2, v, NT)
        delta = jnp.sum(low.astype(F32) * prob_grad, axis=1, keepdims=True)
        score_low = (probs * (prob_grad - delta)).astype(BF16)
        query_grad = (dot(score_low, k, NN) * SCALE).astype(BF16)
        dq[rows, heads[0]] = query_grad[:BLOCK]
        dq[rows, heads[1]] = query_grad[BLOCK:]
        dk_acc[kv, :, span] += dot(q2.T, score_low, NN)
        dv_acc[kv, :, span] += dot(g2.T, low, NN)

    def kv_ready(kv):
        @pl.when(first_core & has_prev)
        def _():
            for which in both:
                kv_arrived(kv, 1, which)
                kv_share(kv, which).start()
            for which in both:
                kv_arrived(kv, 0, which)

        @pl.when(second_core)
        def _():
            for which in both:
                kv_arrived(kv, 1, which)

        @pl.when(second_core & has_prev)
        def _():
            for which in both:
                kv_arrived(kv, 0, which)

    def to_prev(kv, n):
        for which in both:
            grad_prev(kv, n, which).start()

    def grads_out(kv):
        for n in (1, 0):
            cols = slice(WINDOW - (n + 1) * ROWS, WINDOW - n * ROWS)
            halo_out[kv, n, 0] = (dk_acc[kv, :, cols] * SCALE).astype(BF16)
            halo_out[kv, n, 1] = dv_acc[kv, :, cols].astype(BF16)

            if n == 1:
                @pl.when(second_core & has_prev)
                def _():
                    for which in both:
                        grad_mate(kv, 1, which).start()

                @pl.when(first_core & has_prev)
                def _():
                    to_prev(kv, 1)
            else:
                @pl.when(second_core)
                def _():
                    for which in both:
                        grad_mate(kv, 0, which).start()

    def grads_joined(kv):
        @pl.when(first_core & has_prev)
        def _():
            for which in both:
                grad_mate(kv, 1, which).wait_recv()
                term = halo_out[kv, 0, which].astype(F32) + mate_far[kv, which].astype(F32)
                halo_out[kv, 0, which] = term.astype(BF16)
            to_prev(kv, 0)

    for kv in both:
        kv_ready(kv)
        if kv == 0:
            for j in range(8):
                mate_x(j).start()

        def pair(b, carry, kv=kv):
            if kv == 1:
                @pl.when(b == 1)
                def _():
                    grads_joined(0)

            attend(kv, 2 * b)
            attend(kv, 2 * b + 1)
            return carry

        lax.fori_loop(0, ROWS // BLOCK // 2, pair, 0)
        grads_out(kv)
        mate_dq(kv).start()
    grads_joined(1)

    def hop(axis, unit, n, src, dst, device):
        return remote(src, dst, send_sem.at[axis, unit, n], recv_sem.at[axis, unit, n], device)

    def lanes_of(axis, unit):
        return slice(0, HALF) if (axis, unit) == (INPUT, 1) else slice(0, COLS)

    def opposite(axis, unit, way):
        device = (right, left)[way][axis]
        rows, cols = WAY_ROWS[axis][way], lanes_of(axis, unit)
        return hop(axis, unit, way, part.at[axis, unit, 0, rows, cols], relay.at[axis, unit, rows, cols], device)

    def plain(axis, unit, way):
        device = (right, left)[way][axis]
        rows, cols = WAY_ROWS[axis][1 - way], lanes_of(axis, unit)
        return hop(
            axis, unit, 2 + way, part.at[axis, unit, 1 + way, rows, cols], final.at[axis, unit, way, rows, cols], device
        )

    def summed(axis, unit, way):
        device = (right, left)[way][axis]
        rows, cols = WAY_ROWS[axis][way], lanes_of(axis, unit)
        return hop(
            axis, unit, 4 + way, part.at[axis, unit, 1 + way, rows, cols], final.at[axis, unit, way, rows, cols], device
        )

    def crossing(axis, unit, way):
        rows, cols = WAY_ROWS[axis][way], lanes_of(axis, unit)
        slot = unit // 2 if axis == WEIGHT else unit
        return hop(axis, unit, 6 + way, part.at[axis, unit, 3, rows, cols], zland.at[axis, slot, rows, cols], across[axis])

    def early(u):
        return remote(
            part.at[INPUT, 1, u, :, HALF:], zfirst.at[u], early_send.at[u], early_recv.at[u], across[INPUT]
        )

    def join_early():
        for u in range(4):
            early(u).wait_recv()
            kept = part[INPUT, 3, u, :, HALF:].astype(F32)
            part[INPUT, 3, u, :, HALF:] = (kept + zfirst[u].astype(F32)).astype(BF16)

    def target(axis, side, u):
        off = 2 - u + (u // 2) * 3 - (u // 3) * 2
        z = (1 - depth[axis] + side) % 2
        return z * 4 + (place[axis] + off) % 4

    def eager(axis, unit, u):
        @pl.when(u == 0)
        def _():
            for way in both:
                opposite(axis, unit, way).start()

        for way in both:
            @pl.when(u == 1 + way)
            def _():
                plain(axis, unit, way).start()

    def make_weight(unit):
        side, half = unit % 2, unit // 2
        own, other, dims = ((dq, dq_mate, NN), (dkv, dkv_mate, NT))[half]

        def body(u, carry):
            j = target(WEIGHT, side, u)
            product = dot(xt[block_rows(2 * j + core), :], own[...], dims)
            product += dot(x_mate[j], other[...], dims)
            part[WEIGHT, unit, u] = product.astype(BF16)
            return carry

        lax.fori_loop(0, 4, body, 0)

    def make_input(unit):
        side, half = unit // 2, unit % 2

        def body(u, carry):
            j = target(INPUT, side, u) * 2 + half
            product = dot(wq[j], dq[...], NT)
            product += dot(wkv[j], dkv[...], NN)
            part[INPUT, unit, u] = product.astype(BF16)
            if unit == 0:
                eager(INPUT, unit, u)
            return carry

        lax.fori_loop(0, 4, body, 0)

    def send(axis, unit):
        for way in range(2):
            opposite(axis, unit, way).start()
        for way in range(2):
            plain(axis, unit, way).start()

    def forward(axis, unit):
        cols = lanes_of(axis, unit)
        for way in range(2):
            opposite(axis, unit, way).wait_recv()
            rows = WAY_ROWS[axis][way]
            kept = part[axis, unit, 1 + way, rows, cols].astype(F32)
            kept += relay[axis, unit, rows, cols].astype(F32)
            part[axis, unit, 1 + way, rows, cols] = kept.astype(BF16)
            summed(axis, unit, way).start()

    def collected(axis, unit):
        cols = lanes_of(axis, unit)
        for way in range(2):
            plain(axis, unit, way).wait_recv()
            summed(axis, unit, way).wait_recv()
        total = part[axis, unit, 3, :, cols].astype(F32)
        return total + final[axis, unit, 0, :, cols].astype(F32) + final[axis, unit, 1, :, cols].astype(F32)

    def cross(axis, unit):
        part[axis, unit, 3, :, lanes_of(axis, unit)] = collected(axis, unit).astype(BF16)
        for way in range(2):
            crossing(axis, unit, way).start()

    def finish(axis, unit, out):
        total = collected(axis, unit)
        source = unit - 1 if axis == WEIGHT else unit - 2
        slot = source // 2 if axis == WEIGHT else source
        cols = lanes_of(axis, source)
        for way in range(2):
            crossing(axis, source, way).wait_recv()
        out[:, cols] = (total[:, cols] + zland[axis, slot, :, cols].astype(F32)).astype(BF16)
        if cols.stop < COLS:
            out[:, HALF:] = total[:, HALF:].astype(BF16)

    for j in range(8):
        mate_x(j).wait_recv()
    for kv in range(2):
        mate_dq(kv).wait_recv()
    make_weight(0)
    opposite(WEIGHT, 0, 0).start()
    plain(WEIGHT, 0, 0).start()
    make_weight(1)

    own = slice(WINDOW, EXT)
    for kv in both:
        for which in both:
            @pl.when(first_core)
            def _():
                grad_mate(kv, 0, which).wait_recv()

            @pl.when(has_next)
            def _():
                grad_prev(kv, 0, which).wait_recv()

        halo = [halo_in[kv, 0, n].astype(F32) + halo_in[kv, 1, n].astype(F32) for n in both]
        dkv[kv * HD:(kv + 1) * HD, :] = (dk_acc[kv, :, own] * SCALE + halo[0]).astype(BF16)
        dkv[(2 + kv) * HD:(3 + kv) * HD, :] = (dv_acc[kv, :, own] + halo[1]).astype(BF16)
    mate_dkv().start()
    for n in (5, 6, 7):
        load(n).wait()

    make_input(0)
    opposite(WEIGHT, 0, 1).start()
    plain(WEIGHT, 0, 1).start()
    make_input(1)
    for u in range(4):
        early(u).start()
    mate_dkv().wait_recv()
    make_weight(2)
    forward(INPUT, 0)
    send(INPUT, 1)
    forward(WEIGHT, 0)
    send(WEIGHT, 2)
    make_input(2)
    make_weight(3)
    make_input(3)
    cross(INPUT, 0)
    cross(WEIGHT, 0)
    forward(INPUT, 1)
    send(INPUT, 2)
    forward(WEIGHT, 2)
    send(WEIGHT, 1)
    cross(INPUT, 1)
    join_early()
    forward(INPUT, 2)
    send(INPUT, 3)
    cross(WEIGHT, 2)
    forward(WEIGHT, 1)
    send(WEIGHT, 3)
    forward(INPUT, 3)
    forward(WEIGHT, 3)
    finish(WEIGHT, 1, out_q)
    finish(INPUT, 2, out_h.at[:PIECE])
    finish(INPUT, 3, out_h.at[PIECE:])
    finish(WEIGHT, 3, out_kv)

    for kv in both:
        mate_dq(kv).wait_send()
        for which in both:
            @pl.when(has_next)
            def _():
                kv_next(kv, which).wait_send()

            @pl.when(first_core)
            def _():
                kv_mate(kv, which).wait_send()

            @pl.when(first_core & has_prev)
            def _():
                kv_share(kv, which).wait_send()

            @pl.when(second_core)
            def _():
                grad_mate(kv, 0, which).wait_send()

            @pl.when(second_core & has_prev)
            def _():
                grad_mate(kv, 1, which).wait_send()

            @pl.when(first_core & has_prev)
            def _():
                grad_prev(kv, 0, which).wait_send()
                grad_prev(kv, 1, which).wait_send()

    for j in range(8):
        mate_x(j).wait_send()
    mate_dkv().wait_send()
    for u in range(4):
        early(u).wait_send()
    for axis in range(2):
        for unit in range(4):
            for way in range(2):
                opposite(axis, unit, way).wait_send()
                plain(axis, unit, way).wait_send()
                summed(axis, unit, way).wait_send()
                if axis == WEIGHT and unit % 2 == 0:
                    crossing(axis, unit, way).wait_send()
                if axis == INPUT and unit < 2:
                    crossing(axis, unit, way).wait_send()


def whole_step(lengths, x, q, g, k, v, wq, wk, wv):
    vmem = pl.BlockSpec(memory_space=pltpu.VMEM)
    anywhere = pl.BlockSpec(memory_space=pl.ANY)
    dma = pltpu.SemaphoreType.DMA
    piece = (PIECE, COLS)
    return pl.pallas_call(
        step_kernel,
        out_shape=[
            jax.ShapeDtypeStruct((2 * PIECE, ROWS), BF16),
            jax.ShapeDtypeStruct(piece, BF16),
            jax.ShapeDtypeStruct(piece, BF16),
        ],
        in_specs=[pl.BlockSpec(memory_space=pltpu.SMEM)] + [anywhere] * 8,
        out_specs=[vmem] * 3,
        scratch_shapes=[
            pltpu.VMEM((ROWS, D), BF16),
            pltpu.VMEM((D, ROWS), BF16),
            pltpu.VMEM((8, PIECE, ROWS), BF16),
            pltpu.VMEM((ROWS, COLS), BF16),
            pltpu.VMEM((ROWS, COLS), BF16),
            pltpu.VMEM((EXT, 2 * HD), BF16),
            pltpu.VMEM((EXT, 2 * HD), BF16),
            pltpu.VMEM((16, PIECE, COLS), BF16),
            pltpu.VMEM((16, PIECE, COLS), BF16),
            pltpu.VMEM((ROWS // BLOCK, BLOCK, SPAN), F32),
            pltpu.VMEM((2, HD, EXT), F32),
            pltpu.VMEM((2, HD, EXT), F32),
            pltpu.VMEM((ROWS, COLS), BF16),
            pltpu.VMEM((ROWS, COLS), BF16),
            pltpu.VMEM((COLS, ROWS), BF16),
            pltpu.VMEM((COLS, ROWS), BF16),
            pltpu.VMEM((2, 2, 2, HD, ROWS), BF16),
            pltpu.VMEM((2, 2, 2, HD, ROWS), BF16),
            pltpu.VMEM((2, 2, HD, ROWS), BF16),
            pltpu.VMEM((2, 4, 4) + piece, BF16),
            pltpu.VMEM((2, 4) + piece, BF16),
            pltpu.VMEM((2, 4, 2) + piece, BF16),
            pltpu.VMEM((2, 2) + piece, BF16),
            pltpu.VMEM((4, PIECE, HALF), BF16),
            dma((8,)),
            dma((2, 3, 2)),
            dma((2, 2, 2)),
            dma((2, 2, 2)),
            dma((2, 3, 2)),
            dma((11,)),
            dma((11,)),
            dma((2, 4, 8)),
            dma((2, 4, 8)),
            dma((4,)),
            dma((4,)),
        ],
        compiler_params=pltpu.CompilerParams(
            collective_id=1, has_side_effects=True, vmem_limit_bytes=67043328
        ),
        name="step",
    )(lengths, x, q, g, k, v, wq, wk, wv)


def write_kernel(h, q, kv, out_h, out_q, out_k, out_v, h_at, q_at, kv_at, read, write):
    loads = [
        pltpu.make_async_copy(src, dst, read.at[n])
        for n, (src, dst) in enumerate(((h, h_at), (q, q_at), (kv, kv_at)))
    ]
    stores = [
        pltpu.make_async_copy(src, dst, write.at[n])
        for n, (src, dst) in enumerate((
            (h_at, out_h), (q_at, out_q), (kv_at.at[:, :HALF], out_k), (kv_at.at[:, HALF:], out_v),
        ))
    ]
    for copy in loads:
        copy.start()
    for n, needs in enumerate((0, 1, 2, None)):
        if needs is not None:
            loads[needs].wait()
        stores[n].start()
    for copy in stores:
        copy.wait()


def written(h, q, kv):
    anywhere = pl.BlockSpec(memory_space=pl.ANY)
    shapes = ((2 * PIECE, ROWS), (PIECE, COLS), (PIECE, COLS // 2), (PIECE, COLS // 2))
    return pl.pallas_call(
        write_kernel,
        out_shape=[jax.ShapeDtypeStruct(shape, BF16) for shape in shapes],
        in_specs=[anywhere] * 3,
        out_specs=[anywhere] * 4,
        scratch_shapes=[
            pltpu.VMEM((2 * PIECE, ROWS), BF16),
            pltpu.VMEM((PIECE, COLS), BF16),
            pltpu.VMEM((PIECE, COLS), BF16),
            pltpu.SemaphoreType.DMA((3,)),
            pltpu.SemaphoreType.DMA((4,)),
        ],
        name="write",
    )(h, q, kv)


def on_device(layer_input, query, keys, values, out_grad, w_query, w_key, w_value, proof_lengths):
    weights = [w.reshape(16, PIECE, -1) for w in (w_query, w_key, w_value)]
    results = whole_step(proof_lengths, layer_input, query, out_grad, keys, values, *weights)
    input_grad, wq_grad, wk_grad, wv_grad = written(*results)
    return (input_grad.T, wq_grad, wk_grad, wv_grad)


def solution(mesh):
    return jax.shard_map(
        on_device,
        mesh=mesh,
        in_specs=(
            P("seq", None),
            P("seq", "head"),
            P("seq", "head"),
            P("seq", "head"),
            P("seq", "head"),
            P(None, "head"),
            P(None, "head"),
            P(None, "head"),
            P(),
        ),
        out_specs=(P("seq", "head"), P("seq", "head"), P("seq", "head"), P("seq", "head")),
        check_vma=False,
    )
```
